32 devices in a mesh: dp: 2 (over core), row: 4 (over y, x), col: 4 (over z).
Axes of the slice: x: 2, y: 2, z: 4, core: 2. Of those that a mesh axis runs over, the one named last changes fastest.
Arguments:
- inputs: bfloat16 [2048, 1024], P('dp', ('row', 'col')), may hold values from -6 to 6
- first_gain: float32 [1024], P(('row', 'col')), may hold values from 0.25 to 1.75
- first_shift: float32 [1024], P(('row', 'col')), may hold values from -3 to 3
- input_weight: bfloat16 [1024, 3, 1024], P('row', None, 'col'), may hold values from -0.1875 to 0.1875
- input_bias: float32 [2, 1024], P(None, ('col', 'row')), may hold values from -3 to 3
- mixer_weight: bfloat16 [1024, 1024], P('col', 'row'), may hold values from -0.5 to 0.5
- mixer_bias: float32 [1024], P(('row', 'col')), may hold values from -3 to 3
- second_gain: float32 [1024], P(('row', 'col')), may hold values from 0.25 to 1.75
- second_shift: float32 [1024], P(('row', 'col')), may hold values from -3 to 3
- expand_weight: bfloat16 [1024, 4096], P('row', 'col'), may hold values from -0.1875 to 0.1875
- expand_bias: float32 [4096], P(('col', 'row')), may hold values from -3 to 3
- shrink_weight: bfloat16 [4096, 1024], P('col', 'row'), may hold values from -0.09375 to 0.09375
- shrink_bias: float32 [1024], P(('row', 'col')), may hold values from -3 to 3
- cotangent: bfloat16 [2048, 1024], P('dp', ('row', 'col')), may hold values from -6 to 6
Outputs:
- outputs: bfloat16 [2048, 1024], P('dp', ('row', 'col'))
- input_grad: float32 [2048, 1024], P('dp', ('row', 'col'))
- first_gain_grad: float32 [1024], P(('row', 'col'))
- first_shift_grad: float32 [1024], P(('row', 'col'))
- input_weight_grad: float32 [1024, 3, 1024], P('row', None, 'col')
- input_bias_grad: float32 [2, 1024], P(None, ('col', 'row'))
- mixer_weight_grad: float32 [1024, 1024], P('col', 'row')
- mixer_bias_grad: float32 [1024], P(('row', 'col'))
- second_gain_grad: float32 [1024], P(('row', 'col'))
- second_shift_grad: float32 [1024], P(('row', 'col'))
- expand_weight_grad: float32 [1024, 4096], P('row', 'col')
- expand_bias_grad: float32 [4096], P(('col', 'row'))
- shrink_weight_grad: float32 [4096, 1024], P('col', 'row')
- shrink_bias_grad: float32 [1024], P(('row', 'col'))
The draws below stay inside these ranges and needn't reach their ends.
All inputs are finite; a program needn't handle non-finite values.
Results may differ from the reference program's by a relative error of at most 0.014.
Values may be sent and summed in bfloat16 or wider, within the bound.
A program may use at most 64 MiB of HBM per device.

```python
import math
import jax
import jax.numpy as jnp
from jax import lax

D = 1024
H = 16
HD = 64
FF = 4096
LEN = 1024
SEQS = 2
TOKENS = 2048


def levels(stream_key, extent, shards, least, high):
    loudness = 1.0
    for dim, blocks in shards:
        heights = jax.random.uniform(jax.random.fold_in(jax.random.fold_in(stream_key, 6), dim), (blocks,), jnp.float32, least / len(shards), high / len(shards))
        loudness = loudness * jnp.repeat(jnp.exp(heights), extent[dim] // blocks).reshape((-1,) + (1,) * (len(extent) - 1 - dim))
    return loudness


def bell_draw(key, extent, scale, reach, pieces=(), kind=jnp.bfloat16):
    drawn = scale * jax.random.normal(key, extent, jnp.float32)
    if pieces:
        drawn = drawn * levels(key, extent, pieces, -0.22, 0.18)
    return jnp.clip(drawn, -reach, reach).astype(kind)


def setup_inputs(seed: int = 0) -> dict:
    seeds = jax.random.split(jax.random.key(seed), 15)
    return {
        "inputs": bell_draw(seeds[0], (TOKENS, D), 1.0, 6.0, ((0, 2), (1, 16))),
        "first_gain": jnp.clip(1.0 + 0.15 * jax.random.normal(seeds[1], (D,), jnp.float32), 0.25, 1.75),
        "first_shift": bell_draw(seeds[2], (D,), 0.5, 3.0, ((0, 16),), jnp.float32),
        "input_weight": bell_draw(seeds[3], (D, 3, D), D ** -0.5, 0.1875, ((0, 4), (2, 4))),
        "input_bias": bell_draw(seeds[4], (2, D), 0.5, 3.0, ((1, 16),), jnp.float32),
        "mixer_weight": bell_draw(seeds[5], (D, D), (D // 8) ** -0.5, 0.5, ((0, 4), (1, 4))),
        "mixer_bias": bell_draw(seeds[6], (D,), 0.5, 3.0, ((0, 16),), jnp.float32),
        "second_gain": jnp.clip(1.0 + 0.15 * jax.random.normal(seeds[7], (D,), jnp.float32), 0.25, 1.75),
        "second_shift": bell_draw(seeds[8], (D,), 0.5, 3.0, ((0, 16),), jnp.float32),
        "expand_weight": bell_draw(seeds[9], (D, FF), D ** -0.5, 0.1875, ((0, 4), (1, 4))),
        "expand_bias": bell_draw(seeds[10], (FF,), 0.5, 3.0, ((0, 16),), jnp.float32),
        "shrink_weight": bell_draw(seeds[11], (FF, D), FF ** -0.5, 0.09375, ((0, 4), (1, 4))),
        "shrink_bias": bell_draw(seeds[12], (D,), 0.5, 3.0, ((0, 16),), jnp.float32),
        "cotangent": bell_draw(seeds[13], (TOKENS, D), 1.0, 6.0, ((0, 2), (1, 16))),
    }


EPSILON = 1e-05
TANH_FACTOR = math.sqrt(2.0 / math.pi)
MASK_FILL = -1e+30

def rounded(values):
    return lax.optimization_barrier(values.astype(jnp.bfloat16))

def gelu_value(preact):
    tanh_input = TANH_FACTOR * (preact + 0.044715 * preact * preact * preact)
    return 0.5 * preact * (1.0 + jnp.tanh(tanh_input))

def gelu_slope(preact):
    tanh_input = TANH_FACTOR * (preact + 0.044715 * preact * preact * preact)
    tangent = jnp.tanh(tanh_input)
    return 0.5 * (1.0 + tangent) + 0.5 * preact * (1.0 - tangent * tangent) * TANH_FACTOR * (1.0 + 3.0 * 0.044715 * preact * preact)

def normalize(values, gain, shift):
    center = lax.optimization_barrier(jnp.mean(values, axis=1, keepdims=True))
    spread = lax.optimization_barrier(jnp.mean(values * values, axis=1, keepdims=True)) - center * center
    inverse = lax.rsqrt(spread + EPSILON)
    standard = (values - center) * inverse
    return (standard, inverse, (standard * gain + shift).astype(jnp.bfloat16))

def normalize_back(grad_out, standard, inverse, gain):
    scaled = grad_out * gain
    return inverse * (scaled - lax.optimization_barrier(jnp.mean(scaled, axis=1, keepdims=True)) - standard * lax.optimization_barrier(jnp.mean(scaled * standard, axis=1, keepdims=True)))

def one_sequence(params, inputs, cotangent):
    first_gain, first_shift, input_weight, input_bias, mixer_weight, mixer_bias, second_gain, second_shift, expand_weight, expand_bias, shrink_weight, shrink_bias = params
    score_scale = HD ** (-0.5)
    position = jnp.arange(LEN)
    causal = (position[:, None] >= position[None, :])[None]
    values = inputs.astype(jnp.float32)
    first_standard, first_inverse, first_normed = normalize(values, first_gain, first_shift)
    flat_weight = input_weight.reshape(D, 3 * D)
    projected = jnp.dot(first_normed, flat_weight, preferred_element_type=jnp.float32).reshape(LEN, 3, D)
    queries = rounded(projected[:, 0] + input_bias[0])
    key_rows = rounded(projected[:, 1])
    value_rows = rounded(projected[:, 2] + input_bias[1])
    query_heads = queries.astype(jnp.float32).reshape(LEN, H, HD)
    key_heads = key_rows.astype(jnp.float32).reshape(LEN, H, HD)
    value_heads = value_rows.astype(jnp.float32).reshape(LEN, H, HD)
    scores = jnp.einsum('qhd,khd->hqk', query_heads, key_heads) * score_scale
    scores = jnp.where(causal, scores, MASK_FILL)
    row_max = lax.optimization_barrier(jnp.max(scores, axis=2, keepdims=True))
    log_total = row_max + jnp.log(lax.optimization_barrier(jnp.sum(jnp.exp(scores - row_max), axis=2, keepdims=True)))
    weights = jnp.exp(scores - log_total)
    weights_low = rounded(weights).astype(jnp.float32)
    attended = rounded(jnp.einsum('hqk,khd->qhd', weights_low, value_heads)).reshape(LEN, D)
    attention = jnp.dot(attended, mixer_weight, preferred_element_type=jnp.float32) + mixer_bias
    middle = values + attention
    second_standard, second_inverse, second_normed = normalize(middle, second_gain, second_shift)
    preact = jnp.dot(second_normed, expand_weight, preferred_element_type=jnp.float32) + expand_bias
    hidden = gelu_value(preact).astype(jnp.bfloat16)
    branch = jnp.dot(hidden, shrink_weight, preferred_element_type=jnp.float32) + shrink_bias
    outputs = (middle + branch).astype(jnp.bfloat16)
    upstream = cotangent.astype(jnp.float32)
    shrink_bias_grad = lax.optimization_barrier(jnp.sum(upstream, axis=0))
    shrink_weight_grad = jnp.dot(hidden.T, cotangent, preferred_element_type=jnp.float32)
    grad_hidden = jnp.dot(cotangent, shrink_weight.T, preferred_element_type=jnp.float32)
    grad_preact = grad_hidden * gelu_slope(preact)
    expand_bias_grad = lax.optimization_barrier(jnp.sum(grad_preact, axis=0))
    preact_low = grad_preact.astype(jnp.bfloat16)
    expand_weight_grad = jnp.dot(second_normed.T, preact_low, preferred_element_type=jnp.float32)
    grad_second = jnp.dot(preact_low, expand_weight.T, preferred_element_type=jnp.float32)
    second_gain_grad = lax.optimization_barrier(jnp.sum(grad_second * second_standard, axis=0))
    second_shift_grad = lax.optimization_barrier(jnp.sum(grad_second, axis=0))
    grad_middle = upstream + normalize_back(grad_second, second_standard, second_inverse, second_gain)
    mixer_bias_grad = lax.optimization_barrier(jnp.sum(grad_middle, axis=0))
    middle_low = grad_middle.astype(jnp.bfloat16)
    mixer_weight_grad = jnp.dot(attended.T, middle_low, preferred_element_type=jnp.float32)
    grad_attended = rounded(jnp.dot(middle_low, mixer_weight.T, preferred_element_type=jnp.float32))
    grad_heads = grad_attended.astype(jnp.float32).reshape(LEN, H, HD)
    attended_heads = attended.astype(jnp.float32).reshape(LEN, H, HD)
    delta = jnp.transpose(lax.optimization_barrier(jnp.sum(grad_heads * attended_heads, axis=2)))[:, :, None]
    value_grad = jnp.einsum('hqk,qhd->khd', weights_low, grad_heads)
    grad_weights = jnp.einsum('qhd,khd->hqk', grad_heads, value_heads)
    grad_scores = rounded(weights * (grad_weights - delta)).astype(jnp.float32)
    query_grad = jnp.einsum('hqk,khd->qhd', grad_scores, key_heads) * score_scale
    key_grad = jnp.einsum('hqk,qhd->khd', grad_scores, query_heads) * score_scale
    query_grad = query_grad.reshape(LEN, D)
    key_grad = key_grad.reshape(LEN, D)
    value_grad = value_grad.reshape(LEN, D)
    input_bias_grad = jnp.stack([lax.optimization_barrier(jnp.sum(query_grad, axis=0)), lax.optimization_barrier(jnp.sum(value_grad, axis=0))])
    stacked = jnp.stack([query_grad, key_grad, value_grad], axis=1).astype(jnp.bfloat16).reshape(LEN, 3 * D)
    input_weight_grad = jnp.dot(first_normed.T, stacked, preferred_element_type=jnp.float32).reshape(D, 3, D)
    grad_first = jnp.dot(stacked, flat_weight.T, preferred_element_type=jnp.float32)
    first_gain_grad = lax.optimization_barrier(jnp.sum(grad_first * first_standard, axis=0))
    first_shift_grad = lax.optimization_barrier(jnp.sum(grad_first, axis=0))
    input_grad = grad_middle + normalize_back(grad_first, first_standard, first_inverse, first_gain)
    gradients = (first_gain_grad, first_shift_grad, input_weight_grad, input_bias_grad, mixer_weight_grad, mixer_bias_grad, second_gain_grad, second_shift_grad, expand_weight_grad, expand_bias_grad, shrink_weight_grad, shrink_bias_grad)
    return (outputs, input_grad, gradients)

def reference(inputs, first_gain, first_shift, input_weight, input_bias, mixer_weight, mixer_bias, second_gain, second_shift, expand_weight, expand_bias, shrink_weight, shrink_bias, cotangent):
    params = (first_gain, first_shift, input_weight, input_bias, mixer_weight, mixer_bias, second_gain, second_shift, expand_weight, expand_bias, shrink_weight, shrink_bias)
    starting = tuple((jnp.zeros(param.shape, jnp.float32) for param in params))

    def advance(running, sequence_pair):
        outputs, input_grad, fresh = one_sequence(params, sequence_pair[0], sequence_pair[1])
        return (tuple((total + extra for total, extra in zip(running, fresh))), (outputs, input_grad))
    totals, (outputs, input_grad) = lax.scan(advance, starting, (inputs.reshape(SEQS, LEN, D), cotangent.reshape(SEQS, LEN, D)))
    return (outputs.reshape(TOKENS, D), input_grad.reshape(TOKENS, D), totals[0], totals[1], totals[2], totals[3], totals[4], totals[5], totals[6], totals[7], totals[8], totals[9], totals[10], totals[11])
```

```python
import functools
import math

import jax
import jax.numpy as jnp
from jax import lax
from jax.experimental import pallas as pl
from jax.experimental.pallas import tpu as pltpu
from jax.sharding import PartitionSpec as P

D = 1024
HD = 64
LEN = 1024
EPSILON = 1e-05
TANH_FACTOR = math.sqrt(2.0 / math.pi)
MASK_FILL = -1e30
BF = jnp.bfloat16
F32 = jnp.float32
MESH = pl.DeviceIdType.MESH
VMEM = pl.BlockSpec(memory_space=pltpu.VMEM)


def gelu_both(preact):
    square = preact * preact
    tangent = jnp.tanh(TANH_FACTOR * (preact + 0.044715 * square * preact))
    value = 0.5 * preact * (1.0 + tangent)
    slope = 0.5 * (1.0 + tangent) + 0.5 * preact * (1.0 - tangent * tangent) * TANH_FACTOR * (
        1.0 + 3.0 * 0.044715 * square
    )
    return value, slope


def norm_forward(values, gain, shift):
    center = jnp.mean(values, axis=1, keepdims=True)
    squares = jnp.mean(values * values, axis=1, keepdims=True)
    inverse = lax.rsqrt(squares - center * center + EPSILON)
    standard = (values - center) * inverse
    return (standard, inverse, (standard * gain + shift).astype(BF))


def norm_backward(grad_out, standard, inverse, gain):
    scaled = grad_out * gain
    first = jnp.mean(scaled, axis=1, keepdims=True)
    second = jnp.mean(scaled * standard, axis=1, keepdims=True)
    return inverse * (scaled - first - standard * second)


class Exchange:
    def __init__(self, sizes):
        self.sizes = sizes
        self.calls = 0

    def __call__(self, axes, arrays, gather):
        sizes = [self.sizes[a] for a in axes]
        n = math.prod(sizes)
        count = len(arrays)

        def target(index):
            out = {}
            for axis, size in reversed(list(zip(axes, sizes))):
                out[axis] = lax.rem(index, size)
                index = lax.div(index, size)
            return out

        def kernel(*refs):
            ins, outs = refs[:count], refs[count : 2 * count]
            send_sem, recv_sem = refs[2 * count :]
            me = lax.axis_index(axes[0])
            for axis, size in list(zip(axes, sizes))[1:]:
                me = me * size + lax.axis_index(axis)
            barrier = pltpu.get_barrier_semaphore()
            for k in range(1, n):
                pl.semaphore_signal(
                    barrier, inc=1, device_id=target(lax.rem(me + k, n)), device_id_type=MESH
                )
            pl.semaphore_wait(barrier, n - 1)
            copies = []
            for o in range(count):
                for k in range(1, n):
                    peer = lax.rem(me + k, n)
                    copy = pltpu.make_async_remote_copy(
                        src_ref=ins[o] if gather[o] else ins[o].at[peer],
                        dst_ref=outs[o].at[me],
                        send_sem=send_sem.at[o, k],
                        recv_sem=recv_sem.at[o, k],
                        device_id=target(peer),
                        device_id_type=MESH,
                    )
                    copy.start()
                    copies.append(copy)
            for o in range(count):
                outs[o][me] = ins[o][...] if gather[o] else ins[o][me]
            for copy in copies:
                copy.wait()

        out_shape = [
            jax.ShapeDtypeStruct(((n,) + a.shape) if g else a.shape, a.dtype)
            for a, g in zip(arrays, gather)
        ]
        self.calls += 1
        return pl.pallas_call(
            kernel,
            out_shape=out_shape,
            in_specs=[VMEM] * count,
            out_specs=[VMEM] * count,
            scratch_shapes=[
                pltpu.SemaphoreType.DMA((count, n)),
                pltpu.SemaphoreType.DMA((count, n)),
            ],
            compiler_params=pltpu.CompilerParams(
                collective_id=self.calls, has_side_effects=True
            ),
            name=f"exchange_{self.calls}",
        )(*arrays)


def dot(a, b, dims):
    return lax.dot_general(a, b, (dims, ((), ())), preferred_element_type=F32)


NN = ((1,), (0,))
NT = ((1,), (1,))
TN = ((0,), (0,))


def causal_scores(query, keys, offset):
    scores = dot(query, keys, NT) * HD ** (-0.5)
    rows = offset + lax.broadcasted_iota(jnp.int32, scores.shape, 0)
    columns = lax.broadcasted_iota(jnp.int32, scores.shape, 1)
    return jnp.where(rows >= columns, scores, MASK_FILL)


def attend_forward_kernel(q_ref, k_ref, v_ref, out_ref, total_ref, *, block):
    length = q_ref.shape[0]
    for start in range(0, length, block):
        end = start + block
        scores = causal_scores(q_ref[start:end], k_ref[:end], start)
        row_max = jnp.max(scores, axis=1, keepdims=True)
        powers = jnp.exp(scores - row_max)
        row_sum = jnp.sum(powers, axis=1, keepdims=True)
        weights = (powers * (1.0 / row_sum)).astype(BF)
        out_ref[start:end] = dot(weights, v_ref[:end], NN).astype(BF)
        total_ref[start:end] = row_max + jnp.log(row_sum)


def attend_forward(queries, key_rows, value_rows, block=256):
    length = queries.shape[0]
    return pl.pallas_call(
        functools.partial(attend_forward_kernel, block=block),
        out_shape=[
            jax.ShapeDtypeStruct(queries.shape, BF),
            jax.ShapeDtypeStruct((length, 1), F32),
        ],
        in_specs=[VMEM] * 3,
        out_specs=[VMEM] * 2,
        name="attend_forward",
    )(queries, key_rows, value_rows)


def attend_backward_kernel(
    q_ref, k_ref, v_ref, a_ref, total_ref, g_ref, dq_ref, dk_ref, dv_ref, *, block
):
    length = q_ref.shape[0]
    dk_ref[...] = jnp.zeros_like(dk_ref)
    dv_ref[...] = jnp.zeros_like(dv_ref)
    for start in range(0, length, block):
        end = start + block
        grad = g_ref[start:end]
        query = q_ref[start:end]
        delta = jnp.sum(grad.astype(F32) * a_ref[start:end].astype(F32), axis=1, keepdims=True)
        scores = causal_scores(query, k_ref[:end], start)
        weights = jnp.exp(scores - total_ref[start:end])
        dv_ref[:end] += dot(weights.astype(BF), grad, TN)
        grad_weights = dot(grad, v_ref[:end], NT)
        grad_scores = (weights * (grad_weights - delta)).astype(BF)
        dq_ref[start:end] = HD ** (-0.5) * dot(grad_scores, k_ref[:end], NN)
        dk_ref[:end] += HD ** (-0.5) * dot(grad_scores, query, TN)


def attend_backward(*arrays, block=256):
    shape = jax.ShapeDtypeStruct(arrays[0].shape, F32)
    return pl.pallas_call(
        functools.partial(attend_backward_kernel, block=block),
        out_shape=[shape] * 3,
        in_specs=[VMEM] * 6,
        out_specs=[VMEM] * 3,
        name="attend_backward",
    )(*arrays)


def shards(
    sizes,
    inputs,
    first_gain,
    first_shift,
    input_weight,
    input_bias,
    mixer_weight,
    mixer_bias,
    second_gain,
    second_shift,
    expand_weight,
    expand_bias,
    shrink_weight,
    shrink_bias,
    cotangent,
):
    exchange = Exchange(sizes)
    rows, cols = sizes["row"], sizes["col"]
    n = rows * cols
    tokens, wide = inputs.shape
    part, band = tokens // n, tokens // rows
    width = wide * n
    units = input_weight.shape[2]
    head = units // rows
    both = ("row", "col")

    weight_qkv = lax.all_gather(
        input_weight.reshape(input_weight.shape[0], 3 * units), "row", axis=0, tiled=True
    )
    weight_mix = lax.all_gather(mixer_weight, "row", axis=1, tiled=True)
    weight_up = lax.all_gather(expand_weight, "row", axis=0, tiled=True)
    weight_down = lax.all_gather(shrink_weight, "row", axis=1, tiled=True)

    vectors = jnp.concatenate(
        [
            jnp.stack(
                [first_gain, first_shift, mixer_bias, second_gain, second_shift, shrink_bias]
            ).reshape(-1),
            input_bias.reshape(-1),
            expand_bias,
        ]
    )
    lanes = vectors.shape[0] // 6
    x_parts, cot_parts, vectors = exchange(
        both,
        [
            inputs.reshape(n, part, wide),
            cotangent.reshape(n, part, wide),
            vectors.reshape(6, lanes),
        ],
        [False, False, True],
    )
    vectors = vectors.reshape(n, -1)

    def widen(parts):
        return parts.transpose(1, 0, 2).reshape(part, width)

    values = widen(x_parts).astype(F32)
    cot_part = widen(cot_parts)
    upstream = cot_part.astype(F32)
    full = vectors[:, : 6 * wide].reshape(n, 6, wide).transpose(1, 0, 2).reshape(6, 1, width)
    gain1, shift1, bias_mix, gain2, shift2, bias_down = [full[i] for i in range(6)]
    col = lax.axis_index("col")
    mine = lax.dynamic_index_in_dim(
        vectors[:, 6 * wide :].reshape(rows, cols, -1), col, axis=1, keepdims=False
    )
    bias_in = mine[:, : 2 * head].reshape(rows, 2, head).transpose(1, 0, 2).reshape(2, units)
    bias_up = mine[:, 2 * head :].reshape(1, -1)

    standard1, inverse1, normed1 = norm_forward(values, gain1, shift1)
    normed1_band, cot_band = exchange(("col",), [normed1, cot_part], [True, True])
    normed1_band = normed1_band.reshape(band, width)
    cot_band = cot_band.reshape(band, width)

    projected = dot(normed1_band, weight_qkv, NN)
    bias_qkv = jnp.concatenate([bias_in[0], jnp.zeros_like(bias_in[0]), bias_in[1]])
    qkv = (projected + bias_qkv[None]).astype(BF)
    (qkv_heads,) = exchange(
        ("row",), [qkv.reshape(band, 3, rows, head).transpose(2, 1, 0, 3)], [False]
    )
    qkv_heads = qkv_heads.transpose(1, 0, 2, 3).reshape(3, tokens, head)
    queries, key_rows, value_rows = qkv_heads[0], qkv_heads[1], qkv_heads[2]
    attended_head, log_total = attend_forward(queries, key_rows, value_rows)
    (attended,) = exchange(("row",), [attended_head.reshape(rows, band, head)], [False])
    attended = attended.transpose(1, 0, 2).reshape(band, units)

    def sum_col(partial_sum):
        (pieces,) = exchange(("col",), [partial_sum.astype(BF).reshape(cols, part, width)], [False])
        return jnp.sum(pieces.astype(F32), axis=0)

    def gather_col(piece):
        (pieces,) = exchange(("col",), [piece], [True])
        return pieces.reshape(band, width)

    middle = values + sum_col(dot(attended, weight_mix, NN)) + bias_mix
    standard2, inverse2, normed2 = norm_forward(middle, gain2, shift2)
    normed2_band = gather_col(normed2)
    preact = dot(normed2_band, weight_up, NN) + bias_up
    hidden, slope = gelu_both(preact)
    hidden = hidden.astype(BF)
    grad_preact = dot(cot_band, weight_down, NT) * slope
    preact_low = grad_preact.astype(BF)
    grad_second = sum_col(dot(preact_low, weight_up, NT))
    branch = sum_col(dot(hidden, weight_down, NN))
    outputs = (middle + branch + bias_down).astype(BF)

    grad_middle = upstream + norm_backward(grad_second, standard2, inverse2, gain2)
    middle_band = gather_col(grad_middle.astype(BF))
    (grad_attended,) = exchange(
        ("row",),
        [dot(middle_band, weight_mix, NT).astype(BF).reshape(band, rows, head).transpose(1, 0, 2)],
        [False],
    )
    query_grad, key_grad, value_grad = attend_backward(
        queries,
        key_rows,
        value_rows,
        attended_head,
        log_total,
        grad_attended.reshape(tokens, head),
    )
    input_bias_grad = jnp.stack([jnp.sum(query_grad, axis=0), jnp.sum(value_grad, axis=0)])
    stacked = jnp.stack([query_grad, key_grad, value_grad]).astype(BF)
    (stacked,) = exchange(
        ("row",), [stacked.reshape(3, rows, band, head).transpose(1, 0, 2, 3)], [False]
    )
    stacked = stacked.transpose(2, 1, 0, 3).reshape(band, 3 * units)
    grad_first = sum_col(dot(stacked, weight_qkv, NT))
    input_grad = grad_middle + norm_backward(grad_first, standard1, inverse1, gain1)

    def split_rows(grad):
        return grad.astype(BF)

    def over_row(grad, axis):
        return lax.psum_scatter(
            grad.astype(BF), "row", scatter_dimension=axis, tiled=True
        ).astype(F32)

    shrink_weight_grad = over_row(dot(hidden, cot_band, TN), 1)
    expand_weight_grad = over_row(dot(normed2_band, preact_low, TN), 0)
    mixer_weight_grad = over_row(dot(attended, middle_band, TN), 1)
    input_weight_grad = over_row(dot(normed1_band, stacked, TN), 0).reshape(input_weight.shape)

    shared = jnp.stack(
        [
            jnp.sum(grad_first * standard1, axis=0),
            jnp.sum(grad_first, axis=0),
            jnp.sum(grad_middle, axis=0),
            jnp.sum(grad_second * standard2, axis=0),
            jnp.sum(grad_second, axis=0),
            jnp.sum(upstream, axis=0),
        ]
    )
    up_grad = jnp.sum(grad_preact, axis=0)
    out_parts, in_parts, shared, up_parts = exchange(
        both,
        [
            outputs.reshape(part, n, wide).transpose(1, 0, 2),
            input_grad.astype(BF).reshape(part, n, wide).transpose(1, 0, 2),
            shared.reshape(6, n, wide).transpose(1, 0, 2),
            jnp.broadcast_to(up_grad.reshape(rows, 1, 1, -1), (rows, cols, 1, up_grad.shape[0] // rows)).reshape(n, 1, -1),
        ],
        [False] * 4,
    )
    outputs = out_parts.reshape(tokens, wide)
    input_grad = in_parts.reshape(tokens, wide).astype(F32)
    shared = jnp.sum(shared, axis=0)
    expand_bias_grad = jnp.sum(
        lax.dynamic_index_in_dim(
            up_parts.reshape(rows, cols, -1), col, axis=1, keepdims=False
        ),
        axis=0,
    )
    (
        shared,
        input_weight_grad,
        input_bias_grad,
        mixer_weight_grad,
        expand_weight_grad,
        expand_bias_grad,
        shrink_weight_grad,
    ) = lax.psum(
        (
            shared,
            input_weight_grad,
            input_bias_grad,
            mixer_weight_grad,
            expand_weight_grad,
            expand_bias_grad,
            shrink_weight_grad,
        ),
        "dp",
    )
    return (
        outputs,
        input_grad,
        shared[0],
        shared[1],
        input_weight_grad,
        input_bias_grad,
        mixer_weight_grad,
        shared[2],
        shared[3],
        shared[4],
        expand_weight_grad,
        expand_bias_grad,
        shrink_weight_grad,
        shared[5],
    )


def solution(mesh):
    in_specs = (
        P("dp", ("row", "col")),
        P(("row", "col")),
        P(("row", "col")),
        P("row", None, "col"),
        P(None, ("col", "row")),
        P("col", "row"),
        P(("row", "col")),
        P(("row", "col")),
        P(("row", "col")),
        P("row", "col"),
        P(("col", "row")),
        P("col", "row"),
        P(("row", "col")),
        P("dp", ("row", "col")),
    )
    out_specs = (
        P("dp", ("row", "col")),
        P("dp", ("row", "col")),
        P(("row", "col")),
        P(("row", "col")),
        P("row", None, "col"),
        P(None, ("col", "row")),
        P("col", "row"),
        P(("row", "col")),
        P(("row", "col")),
        P(("row", "col")),
        P("row", "col"),
        P(("col", "row")),
        P("col", "row"),
        P(("row", "col")),
    )
    body = functools.partial(shards, dict(mesh.shape))
    return jax.shard_map(
        body, mesh=mesh, in_specs=in_specs, out_specs=out_specs, check_vma=False
    )
```

```python
import functools
import math

import jax
import jax.numpy as jnp
from jax import lax
from jax.experimental import pallas as pl
from jax.experimental.pallas import tpu as pltpu
from jax.sharding import PartitionSpec as P

D = 1024
HD = 64
LEN = 1024
EPSILON = 1e-05
TANH_FACTOR = math.sqrt(2.0 / math.pi)
MASK_FILL = -1e30
BF = jnp.bfloat16
F32 = jnp.float32
MESH = pl.DeviceIdType.MESH
VMEM = pl.BlockSpec(memory_space=pltpu.VMEM)


def gelu_both(preact):
    square = preact * preact
    tangent = jnp.tanh(TANH_FACTOR * (preact + 0.044715 * square * preact))
    value = 0.5 * preact * (1.0 + tangent)
    slope = 0.5 * (1.0 + tangent) + 0.5 * preact * (1.0 - tangent * tangent) * TANH_FACTOR * (
        1.0 + 3.0 * 0.044715 * square
    )
    return value, slope


def norm_forward(values, gain, shift):
    center = jnp.mean(values, axis=1, keepdims=True)
    squares = jnp.mean(values * values, axis=1, keepdims=True)
    inverse = lax.rsqrt(squares - center * center + EPSILON)
    standard = (values - center) * inverse
    return (standard, inverse, (standard * gain + shift).astype(BF))


def norm_backward(grad_out, standard, inverse, gain):
    scaled = grad_out * gain
    first = jnp.mean(scaled, axis=1, keepdims=True)
    second = jnp.mean(scaled * standard, axis=1, keepdims=True)
    return inverse * (scaled - first - standard * second)


def whole(ref, index):
    return ref


def lead(ref, index):
    return ref.at[index]


def second(ref, index):
    return ref.at[:, index]


def lanes_of(size):
    return lambda ref, index: ref.at[:, pl.ds(pl.multiple_of(index * size, size), size)]


class Exchange:
    def __init__(self, sizes):
        self.sizes = dict(sizes, pair=2)
        self.calls = 0

    def __call__(self, *items):
        count = len(items)
        groups = []
        for axes in sorted({item[0] for item in items}, key=len, reverse=True):
            if not any(set(axes) < set(other) for other in groups):
                groups.append(axes)
        most = max(math.prod(self.sizes[a] for a in item[0]) for item in items)

        def size_of(axes):
            return math.prod(self.sizes[a] for a in axes)

        def position(axes):
            me = 0
            for axis in axes:
                if axis == "pair":
                    me = lax.rem(lax.axis_index("dp"), 2)
                else:
                    me = me * self.sizes[axis] + lax.axis_index(axis)
            return me

        def target(axes, index):
            out = {}
            for axis in reversed(axes):
                if axis == "pair":
                    dp = lax.axis_index("dp")
                    out["dp"] = dp - lax.rem(dp, 2) + index
                else:
                    out[axis] = lax.rem(index, self.sizes[axis])
                    index = lax.div(index, self.sizes[axis])
            return out

        def kernel(*refs):
            ins, outs = refs[:count], refs[count : 2 * count]
            send_sem, recv_sem, own_sem = refs[2 * count :]
            barrier = pltpu.get_barrier_semaphore()
            greeted = 0
            for axes in groups:
                n, me = size_of(axes), position(axes)
                for k in range(1, n):
                    pl.semaphore_signal(
                        barrier,
                        inc=1,
                        device_id=target(axes, lax.rem(me + k, n)),
                        device_id_type=MESH,
                    )
                greeted += n - 1
            pl.semaphore_wait(barrier, greeted)
            copies = []
            for o, (axes, _, _, src, dst) in enumerate(items):
                n, me = size_of(axes), position(axes)
                for k in range(1, n):
                    peer = lax.rem(me + k, n)
                    copies.append(
                        pltpu.make_async_remote_copy(
                            src_ref=src(ins[o], peer),
                            dst_ref=dst(outs[o], me),
                            send_sem=send_sem.at[o, k],
                            recv_sem=recv_sem.at[o, k],
                            device_id=target(axes, peer),
                            device_id_type=MESH,
                        )
                    )
                    copies[-1].start()
            for o, (axes, _, _, src, dst) in enumerate(items):
                me = position(axes)
                copies.append(
                    pltpu.make_async_copy(src(ins[o], me), dst(outs[o], me), own_sem.at[o])
                )
                copies[-1].start()
            for copy in copies:
                copy.wait()

        self.calls += 1
        return pl.pallas_call(
            kernel,
            out_shape=[jax.ShapeDtypeStruct(i[2], i[1].dtype) for i in items],
            in_specs=[VMEM] * count,
            out_specs=[VMEM] * count,
            scratch_shapes=[
                pltpu.SemaphoreType.DMA((count, most)),
                pltpu.SemaphoreType.DMA((count, most)),
                pltpu.SemaphoreType.DMA((count,)),
            ],
            compiler_params=pltpu.CompilerParams(
                collective_id=self.calls, has_side_effects=True
            ),
            name=f"exchange_{self.calls}",
        )(*[i[1] for i in items])


def dot(a, b, dims):
    return lax.dot_general(a, b, (dims, ((), ())), preferred_element_type=F32)


NN = ((1,), (0,))
NT = ((1,), (1,))
TN = ((0,), (0,))


def causal_scores(query, keys, offset):
    scores = dot(query, keys, NT) * HD ** (-0.5)
    rows = offset + lax.broadcasted_iota(jnp.int32, scores.shape, 0)
    columns = lax.broadcasted_iota(jnp.int32, scores.shape, 1)
    return jnp.where(rows >= columns, scores, MASK_FILL)


def attend_forward_kernel(q_ref, k_ref, v_ref, out_ref, total_ref, *, block):
    length = q_ref.shape[0]
    for start in range(0, length, block):
        end = start + block
        scores = causal_scores(q_ref[start:end], k_ref[:end], start)
        row_max = jnp.max(scores, axis=1, keepdims=True)
        powers = jnp.exp(scores - row_max)
        row_sum = jnp.sum(powers, axis=1, keepdims=True)
        weights = (powers * (1.0 / row_sum)).astype(BF)
        out_ref[start:end] = dot(weights, v_ref[:end], NN).astype(BF)
        total_ref[start:end] = row_max + jnp.log(row_sum)


def attend_forward(queries, key_rows, value_rows, block=256):
    length = queries.shape[0]
    return pl.pallas_call(
        functools.partial(attend_forward_kernel, block=block),
        out_shape=[
            jax.ShapeDtypeStruct(queries.shape, BF),
            jax.ShapeDtypeStruct((length, 1), F32),
        ],
        in_specs=[VMEM] * 3,
        out_specs=[VMEM] * 2,
        name="attend_forward",
    )(queries, key_rows, value_rows)


def attend_backward_kernel(
    q_ref, k_ref, v_ref, a_ref, total_ref, g_ref, dq_ref, dk_ref, dv_ref, *, block
):
    length = q_ref.shape[0]
    dk_ref[...] = jnp.zeros_like(dk_ref)
    dv_ref[...] = jnp.zeros_like(dv_ref)
    for start in range(0, length, block):
        end = start + block
        grad = g_ref[start:end]
        query = q_ref[start:end]
        delta = jnp.sum(grad.astype(F32) * a_ref[start:end].astype(F32), axis=1, keepdims=True)
        scores = causal_scores(query, k_ref[:end], start)
        weights = jnp.exp(scores - total_ref[start:end])
        dv_ref[:end] += dot(weights.astype(BF), grad, TN)
        grad_weights = dot(grad, v_ref[:end], NT)
        grad_scores = (weights * (grad_weights - delta)).astype(BF)
        dq_ref[start:end] = HD ** (-0.5) * dot(grad_scores, k_ref[:end], NN)
        dk_ref[:end] += HD ** (-0.5) * dot(grad_scores, query, TN)


def attend_backward(*arrays, block=256):
    shape = jax.ShapeDtypeStruct(arrays[0].shape, F32)
    return pl.pallas_call(
        functools.partial(attend_backward_kernel, block=block),
        out_shape=[shape] * 3,
        in_specs=[VMEM] * 6,
        out_specs=[VMEM] * 3,
        name="attend_backward",
    )(*arrays)


def shards(
    sizes,
    inputs,
    first_gain,
    first_shift,
    input_weight,
    input_bias,
    mixer_weight,
    mixer_bias,
    second_gain,
    second_shift,
    expand_weight,
    expand_bias,
    shrink_weight,
    shrink_bias,
    cotangent,
):
    exchange = Exchange(sizes)
    rows, cols = sizes["row"], sizes["col"]
    n = rows * cols
    tokens, wide = inputs.shape
    part, band = tokens // n, tokens // rows
    width = wide * n
    deep, units = input_weight.shape[0], input_weight.shape[2]
    ff = expand_weight.shape[1]
    head = units // rows
    both, row, col, pair = ("row", "col"), ("row",), ("col",), ("pair",)
    pair_me = lax.rem(lax.axis_index("dp"), 2)

    def swap(axes, array):
        return (axes, array, array.shape, lead, lead)

    def gather(axes, array):
        size = math.prod(exchange.sizes[a] for a in axes)
        return (axes, array, (size,) + array.shape, whole, lead)

    def my_half(ref, index):
        return ref.at[lax.rem(lax.axis_index("dp"), 2)]

    def rows_start(weight):
        d, w = weight.shape
        return (row, weight.reshape(2, d // 2, w), (rows, d // 2, w), my_half, lead)

    def rows_finish(half):
        _, d, w = half.shape
        return (pair, half, (rows, 2, d, w), whole, second)

    def lanes_start(weight):
        d, w = weight.shape
        return (row, weight.reshape(2, d // 2, w), (d // 2, rows * w), my_half, lanes_of(w))

    def lanes_finish(half):
        return gather(pair, half)

    def grad_rows_pair(grad):
        d, w = grad.shape
        return (pair, grad.astype(BF), (2, d, w // 2), lanes_of(w // 2), lead)

    def grad_rows_send(pieces):
        half = jnp.sum(pieces.astype(F32), axis=0).astype(BF)
        d, w = half.shape
        return swap(row, half.reshape(rows, d // rows, w))

    def grad_rows_finish(pieces):
        half = jnp.sum(pieces.astype(F32), axis=0)
        d, w = half.shape
        return (pair, half, (d, 2 * w), whole, lanes_of(w))

    def grad_lanes_pair(grad):
        d, w = grad.shape
        return swap(pair, grad.astype(BF).reshape(2, d // 2, w))

    def grad_lanes_send(pieces):
        half = jnp.sum(pieces.astype(F32), axis=0).astype(BF)
        d, w = half.shape
        return (row, half, (rows, d, w // rows), lanes_of(w // rows), lead)

    def grad_lanes_finish(pieces):
        return gather(pair, jnp.sum(pieces.astype(F32), axis=0))

    def scatter_col(partial_sum):
        return swap(col, partial_sum.astype(BF).reshape(cols, -1, width))

    def total(pieces):
        return jnp.sum(pieces.astype(F32), axis=0)

    vectors = jnp.concatenate(
        [
            jnp.stack(
                [first_gain, first_shift, mixer_bias, second_gain, second_shift, shrink_bias]
            ).reshape(-1),
            input_bias.reshape(-1),
            expand_bias,
        ]
    )
    x_parts, cot_parts, vectors, qkv_half = exchange(
        swap(both, inputs.reshape(n, part, wide)),
        swap(both, cotangent.reshape(n, part, wide)),
        gather(both, vectors.reshape(6, -1)),
        rows_start(input_weight.reshape(deep, 3 * units)),
    )
    vectors = vectors.reshape(n, -1)

    def widen(parts):
        return parts.transpose(1, 0, 2).reshape(part, width)

    values = widen(x_parts).astype(F32)
    cot_part = widen(cot_parts)
    upstream = cot_part.astype(F32)
    full = vectors[:, : 6 * wide].reshape(n, 6, wide).transpose(1, 0, 2).reshape(6, 1, width)
    gain1, shift1, bias_mix, gain2, shift2, bias_down = [full[i] for i in range(6)]
    col_me = lax.axis_index("col")
    mine = lax.dynamic_index_in_dim(
        vectors[:, 6 * wide :].reshape(rows, cols, -1), col_me, axis=1, keepdims=False
    )
    bias_in = mine[:, : 2 * head].reshape(rows, 2, head).transpose(1, 0, 2).reshape(2, units)
    bias_up = mine[:, 2 * head :].reshape(1, -1)

    standard1, inverse1, normed1 = norm_forward(values, gain1, shift1)
    normed1_band, weight_qkv, mix_half, up_half = exchange(
        gather(col, normed1),
        rows_finish(qkv_half),
        lanes_start(mixer_weight),
        rows_start(expand_weight),
    )
    normed1_band = normed1_band.reshape(band, width)
    weight_qkv = weight_qkv.reshape(width, 3 * units)

    projected = dot(normed1_band, weight_qkv, NN)
    bias_qkv = jnp.concatenate([bias_in[0], jnp.zeros_like(bias_in[0]), bias_in[1]])
    qkv = (projected + bias_qkv[None]).astype(BF)
    qkv_heads, weight_mix, weight_up, cot_first = exchange(
        swap(row, qkv.reshape(band, 3, rows, head).transpose(2, 1, 0, 3)),
        lanes_finish(mix_half),
        rows_finish(up_half),
        gather(col, cot_part[: part // 2]),
    )
    weight_mix = weight_mix.reshape(units, width)
    weight_up = weight_up.reshape(width, ff)
    qkv_heads = qkv_heads.transpose(1, 0, 2, 3).reshape(3, tokens, head)
    queries, key_rows, value_rows = qkv_heads[0], qkv_heads[1], qkv_heads[2]
    attended_head, log_total = attend_forward(queries, key_rows, value_rows)
    attended, cot_second = exchange(
        swap(row, attended_head.reshape(rows, band, head)),
        gather(col, cot_part[part // 2 :]),
    )
    attended = attended.transpose(1, 0, 2).reshape(band, units)
    cot_band = jnp.concatenate([cot_first, cot_second], axis=1).reshape(band, width)

    attention, down_half = exchange(
        scatter_col(dot(attended, weight_mix, NN)), lanes_start(shrink_weight)
    )
    middle = values + total(attention) + bias_mix
    standard2, inverse2, normed2 = norm_forward(middle, gain2, shift2)
    normed2_band, weight_down = exchange(gather(col, normed2), lanes_finish(down_half))
    normed2_band = normed2_band.reshape(band, width)
    weight_down = weight_down.reshape(ff, width)
    preact = dot(normed2_band, weight_up, NN) + bias_up
    hidden, slope = gelu_both(preact)
    hidden = hidden.astype(BF)
    grad_preact = dot(cot_band, weight_down, NT) * slope
    preact_low = grad_preact.astype(BF)
    grad_second, down_pair, up_pair = exchange(
        scatter_col(dot(preact_low, weight_up, NT)),
        grad_lanes_pair(dot(hidden, cot_band, TN)),
        grad_rows_pair(dot(normed2_band, preact_low, TN)),
    )
    grad_second = total(grad_second)
    grad_middle = upstream + norm_backward(grad_second, standard2, inverse2, gain2)
    middle_band, down_pieces = exchange(
        gather(col, grad_middle.astype(BF)), grad_lanes_send(down_pair)
    )
    middle_band = middle_band.reshape(band, width)
    branch = dot(hidden, weight_down, NN).astype(BF).reshape(cols, part, width)
    grad_attended, branch_first, mix_pair = exchange(
        swap(
            row,
            dot(middle_band, weight_mix, NT)
            .astype(BF)
            .reshape(band, rows, head)
            .transpose(1, 0, 2),
        ),
        swap(col, branch[:, : part // 2]),
        grad_lanes_pair(dot(attended, middle_band, TN)),
    )
    query_grad, key_grad, value_grad = attend_backward(
        queries,
        key_rows,
        value_rows,
        attended_head,
        log_total,
        grad_attended.reshape(tokens, head),
    )
    input_bias_grad = jnp.stack([jnp.sum(query_grad, axis=0), jnp.sum(value_grad, axis=0)])
    stacked = jnp.stack([query_grad, key_grad, value_grad]).astype(BF)
    stacked, branch_second, mix_pieces = exchange(
        swap(row, stacked.reshape(3, rows, band, head).transpose(1, 0, 2, 3)),
        swap(col, branch[:, part // 2 :]),
        grad_lanes_send(mix_pair),
    )
    stacked = stacked.transpose(2, 1, 0, 3).reshape(band, 3 * units)
    branch = jnp.concatenate([total(branch_first), total(branch_second)], axis=0)
    outputs = (middle + branch + bias_down).astype(BF)
    grad_first, up_pieces, in_pair = exchange(
        scatter_col(dot(stacked, weight_qkv, NT)),
        grad_rows_send(up_pair),
        grad_rows_pair(dot(normed1_band, stacked, TN)),
    )
    grad_first = total(grad_first)
    input_grad = grad_middle + norm_backward(grad_first, standard1, inverse1, gain1)

    shared = jnp.stack(
        [
            jnp.sum(grad_first * standard1, axis=0),
            jnp.sum(grad_first, axis=0),
            jnp.sum(grad_middle, axis=0),
            jnp.sum(grad_second * standard2, axis=0),
            jnp.sum(grad_second, axis=0),
            jnp.sum(upstream, axis=0),
        ]
    )
    up_bias = jnp.sum(grad_preact, axis=0).reshape(rows, 1, -1)
    (
        out_parts,
        in_parts,
        shared,
        up_bias,
        in_pieces,
        down_grad,
        up_grad,
        mix_grad,
    ) = exchange(
        swap(both, outputs.reshape(part, n, wide).transpose(1, 0, 2)),
        swap(both, input_grad.astype(BF).reshape(part, n, wide).transpose(1, 0, 2)),
        swap(both, shared.reshape(6, n, wide).transpose(1, 0, 2)),
        swap(row, up_bias),
        grad_rows_send(in_pair),
        grad_lanes_finish(down_pieces),
        grad_rows_finish(up_pieces),
        grad_lanes_finish(mix_pieces),
    )
    outputs = out_parts.reshape(tokens, wide)
    input_grad = in_parts.reshape(tokens, wide).astype(F32)
    small = jnp.concatenate(
        [
            jnp.sum(shared, axis=0).reshape(-1),
            input_bias_grad.reshape(-1),
            jnp.sum(up_bias, axis=0).reshape(-1),
        ]
    )
    in_grad, small = exchange(grad_rows_finish(in_pieces), gather(pair, small.reshape(6, -1)))
    small = jnp.sum(small, axis=0).reshape(-1)
    grads = (small, in_grad, mix_grad, up_grad, down_grad)
    if sizes["dp"] > 2:
        groups = [list(range(i, sizes["dp"], 2)) for i in range(2)]
        grads = lax.psum(grads, "dp", axis_index_groups=groups)
    small, in_grad, mix_grad, up_grad, down_grad = grads
    shared = small[: 6 * wide].reshape(6, wide)
    return (
        outputs,
        input_grad,
        shared[0],
        shared[1],
        in_grad.reshape(input_weight.shape),
        small[6 * wide : 6 * wide + 2 * head].reshape(2, head),
        mix_grad.reshape(mixer_weight.shape),
        shared[2],
        shared[3],
        shared[4],
        up_grad,
        small[6 * wide + 2 * head :],
        down_grad.reshape(shrink_weight.shape),
        shared[5],
    )


def solution(mesh):
    in_specs = (
        P("dp", ("row", "col")),
        P(("row", "col")),
        P(("row", "col")),
        P("row", None, "col"),
        P(None, ("col", "row")),
        P("col", "row"),
        P(("row", "col")),
        P(("row", "col")),
        P(("row", "col")),
        P("row", "col"),
        P(("col", "row")),
        P("col", "row"),
        P(("row", "col")),
        P("dp", ("row", "col")),
    )
    out_specs = (
        P("dp", ("row", "col")),
        P("dp", ("row", "col")),
        P(("row", "col")),
        P(("row", "col")),
        P("row", None, "col"),
        P(None, ("col", "row")),
        P("col", "row"),
        P(("row", "col")),
        P(("row", "col")),
        P(("row", "col")),
        P("row", "col"),
        P(("col", "row")),
        P("col", "row"),
        P(("row", "col")),
    )
    body = functools.partial(shards, dict(mesh.shape))
    return jax.shard_map(
        body, mesh=mesh, in_specs=in_specs, out_specs=out_specs, check_vma=False
    )
```
